32 devices in a mesh: ord: 4 (over x, core), blk: 8 (over z, y).
Axes of the slice: x: 2, y: 2, z: 4, core: 2. Of those that a mesh axis runs over, the one named last changes fastest.
Arguments:
- coefficients: bfloat16 [32, 2, 256, 4096], P('ord', None, None, 'blk'), may hold values from -1.0546875 to 1.0546875
- leaf_factors: bfloat16 [32, 128, 4096], P('ord', None, 'blk'), may hold values from -0.25 to 0.25
- level_interpolants: bfloat16 [3, 2, 32, 128, 1024], P(None, None, 'ord', None, 'blk'), may hold values from -0.375 to 0.375
- latitude_factors: bfloat16 [32, 5120, 128], P('ord', 'blk'), may hold values from -0.5 to 0.5
- order_ids: int32 [32], replicated, may hold values from 0 to 8191, as said below
Outputs:
- products: bfloat16 [256, 128, 5120], P(None, 'ord', 'blk')
The draws below stay inside these ranges and needn't reach their ends.
Inputs may be any that keep to these rules, and one draw needn't show every extreme that they name: `order_ids`: the slots hold distinct orders of the truncation.
All inputs are finite; a program needn't handle non-finite values.
Results may differ from the reference program's by a relative error of at most 0.011.
Values may be sent and summed in bfloat16 or wider, within the bound.
A program may use at most 128 MiB of HBM per device.

```python
import math
import jax
import jax.numpy as jnp
import numpy as np
from jax import lax

FIELDS = 256
LEAF = 512
RANK = 128
PERIOD = 16384
ORDER_RANGE = 8192
NLON = 256
LEVELS = 3
LAT_DEV = 640
ORDERS = 32
DEGREES = 4096
LATS = 5120
BLK_RANKS = 1024
PAIRS = 128
N_BLK = 8


def draw_order_ids(key, part):
    selected_block = jax.random.permutation(jax.random.fold_in(key, 7), ORDER_RANGE)
    return selected_block[:ORDERS].astype(jnp.int32)


def shard_levels(rng, shape, split, smallest, largest):
    level = 1.0
    for position, blocks in split:
        draws = jax.random.uniform(jax.random.fold_in(jax.random.fold_in(rng, 6), position), (blocks,), jnp.float32, smallest / len(split), largest / len(split))
        level = level * jnp.repeat(jnp.exp(draws), shape[position] // blocks).reshape((-1,) + (1,) * (len(shape) - 1 - position))
    return level


def scatter_about(rng, extent, deviation, bound, split=(), kind=jnp.bfloat16):
    values = jax.random.normal(rng, extent, jnp.float32) * deviation
    if len(split) > 0:
        values = shard_levels(rng, extent, split, -0.22, 0.18) * values
    return jnp.clip(values, min=-bound, max=bound).astype(kind)


def setup_inputs(seed: int = 0) -> dict:
    key_list = jax.random.split(jax.random.key(seed), 6)
    coefficients = scatter_about(key_list[0], (ORDERS, 2, FIELDS, DEGREES), (0.5 * ORDERS ** -0.5), 1.0546875, ((0, 4), (3, 8)))
    leaf_factors = scatter_about(key_list[1], (ORDERS, RANK, DEGREES), LEAF ** -0.5, 0.25, ((0, 4), (2, 8)))
    level_interpolants = scatter_about(key_list[2], (LEVELS, 2, ORDERS, RANK, BLK_RANKS), (2 * RANK) ** -0.5, 0.375, ((2, 4), (4, 8)))
    latitude_factors = scatter_about(key_list[3], (ORDERS, LATS, RANK), RANK ** -0.5, 0.5, ((0, 4), (1, 8)))
    order_ids = draw_order_ids(jax.random.fold_in(key_list[5], 71), 0)
    return {"coefficients": coefficients, "leaf_factors": leaf_factors, "level_interpolants": level_interpolants, "latitude_factors": latitude_factors, "order_ids": order_ids}


def synthesis_table(order_ids, count, period):
    steps = jnp.arange(count, dtype=jnp.int32)
    phase = ((order_ids[:, None].astype(jnp.int32) * steps[None, :]) % period).astype(jnp.float32) * (2.0 * math.pi / period)
    weight = jnp.where(order_ids == 0, 1.0, 2.0).astype(jnp.float32)[:, None]
    table = jnp.stack([weight * jnp.cos(phase), -weight * jnp.sin(phase)], axis=1)
    return table.astype(jnp.bfloat16)


def reference(coefficients, leaf_factors, level_interpolants, latitude_factors, order_ids):
    partner_lists = [np.arange(N_BLK) ^ (N_BLK >> (k + 1)) for k in range(LEVELS)]

    def per_order(items):
        coef, leafm, levm = items
        flat = coef.astype(jnp.float32).reshape(2 * FIELDS, N_BLK, LEAF)
        leaves = leafm.astype(jnp.float32).reshape(RANK, N_BLK, LEAF)
        combined_sum = jnp.einsum('cjl,rjl->cjr', flat, leaves).astype(jnp.bfloat16)
        levels = levm.astype(jnp.float32).reshape(LEVELS, 2, RANK, N_BLK, RANK)
        for k in range(LEVELS):
            partner_block = combined_sum[:, partner_lists[k], :]
            mixed = jnp.einsum('cjr,sjr->cjs', combined_sum.astype(jnp.float32), levels[k, 0])
            mixed = mixed + jnp.einsum('cjr,sjr->cjs', partner_block.astype(jnp.float32), levels[k, 1])
            combined_sum = mixed.astype(jnp.bfloat16)
        return combined_sum

    combined_sum = lax.map(per_order, (coefficients, leaf_factors, jnp.moveaxis(level_interpolants, 2, 0)))
    table = synthesis_table(order_ids, NLON, PERIOD).astype(jnp.float32)
    by_block = jnp.moveaxis(combined_sum, 2, 0)
    lat_blocks = jnp.moveaxis(latitude_factors.reshape(ORDERS, N_BLK, LAT_DEV, RANK), 1, 0)

    def per_block(items):
        red, lat = items
        values = jnp.einsum('mcr,mlr->mcl', red.astype(jnp.float32), lat.astype(jnp.float32))
        values = values.astype(jnp.bfloat16).reshape(ORDERS, 2, FIELDS, LAT_DEV)
        grid = jnp.einsum('mrk,mrfl->kfl', table, values.astype(jnp.float32))
        grid = grid.reshape(NLON, PAIRS, 2, LAT_DEV)
        return (grid[:, :, 0, :] * grid[:, :, 1, :]).astype(jnp.bfloat16)

    block_list = lax.map(per_block, (by_block, lat_blocks))
    return jnp.transpose(block_list, (1, 2, 0, 3)).reshape(NLON, PAIRS, LATS)
```

```python
import functools
import math

import jax
import jax.numpy as jnp
from jax import lax
from jax.experimental import pallas as pl
from jax.experimental.pallas import tpu as pltpu
from jax.sharding import PartitionSpec as P

PERIOD = 16384
NLON = 256
LANES = 128
WINDOW = 2
LEVEL_LAG = 1
MESH = pl.DeviceIdType.MESH
NT = (((1,), (1,)), ((), ()))


def synthesis_table(order_ids, count, period):
    steps = jnp.arange(count, dtype=jnp.int32)
    phase = (steps[:, None] * order_ids[None, :] % period).astype(jnp.float32) * (
        2.0 * math.pi / period
    )
    weight = jnp.where(order_ids == 0, 1.0, 2.0).astype(jnp.float32)[None, :]
    table = jnp.stack([weight * jnp.cos(phase), -weight * jnp.sin(phase)], axis=2)
    return table.astype(jnp.bfloat16).reshape(count, -1)


def butterfly_kernel(
    n_ord, n_blk, coef_hbm, leaf_hbm, interp_hbm, lat_hbm,
    rows_out, lat_out,
    coef, leaf, interp, lat, own, came,
    in_sem, level_send, level_recv, group_send, group_recv, own_sem,
    lat_send, lat_recv, lat_pass,
):
    me_ord, me_blk = lax.axis_index("ord"), lax.axis_index("blk")
    orders, columns, _ = coef.shape
    levels = interp.shape[0]
    parts, _, group, rank = rows_out.shape[1], None, rows_out.shape[2], rows_out.shape[3]

    lat_in = pltpu.make_async_copy(lat_hbm, lat, in_sem.at[2, 0])
    interp_in = pltpu.make_async_copy(interp_hbm, interp, in_sem.at[2, 1])

    def order_in(i):
        return (
            pltpu.make_async_copy(coef_hbm.at[i], coef.at[i], in_sem.at[0, i]),
            pltpu.make_async_copy(leaf_hbm.at[i], leaf.at[i], in_sem.at[1, i]),
        )

    for i in range(orders):
        for copy in order_in(i):
            copy.start()
        if i == 1:
            lat_in.start()
            interp_in.start()

    barrier = pltpu.get_barrier_semaphore()
    partners = [me_blk ^ (n_blk >> (k + 1)) for k in range(levels)]
    for k in range(levels):
        pl.semaphore_signal(barrier, inc=1, device_id={"blk": partners[k]}, device_id_type=MESH)
    peers = [lax.rem(me_ord + d, n_ord) for d in range(1, n_ord)]
    for peer in peers:
        pl.semaphore_signal(barrier, inc=1, device_id={"ord": peer}, device_id_type=MESH)
    pl.semaphore_wait(barrier, levels + n_ord - 1)

    def level_copy(k, i):
        return pltpu.make_async_remote_copy(
            src_ref=own.at[k, i], dst_ref=came.at[k, i],
            send_sem=level_send.at[k, i], recv_sem=level_recv.at[k, i],
            device_id={"blk": partners[k]}, device_id_type=MESH,
        )

    def group_copy(i, d):
        peer = lax.rem(me_ord + d, n_ord)
        return pltpu.make_async_remote_copy(
            src_ref=own_groups(i, peer), dst_ref=rows_out.at[me_ord * orders + i],
            send_sem=group_send.at[i, d], recv_sem=group_recv.at[i, d],
            device_id={"ord": peer}, device_id_type=MESH,
        )

    def own_groups(i, g):
        return own.at[levels, i].reshape(parts, n_ord, group, rank).at[:, g]

    def own_copy(i):
        return pltpu.make_async_copy(
            own_groups(i, me_ord), rows_out.at[me_ord * orders + i], own_sem.at[i]
        )

    def lat_rows(o):
        return lat_out.at[pl.ds(o * orders, orders)]

    half = n_ord // 2
    mate = me_ord ^ 1

    def lat_copy(d):
        target = mate if d == 0 else lax.rem(me_ord + 2 * d, n_ord)
        return pltpu.make_async_remote_copy(
            src_ref=lat, dst_ref=lat_rows(me_ord),
            send_sem=lat_send.at[d], recv_sem=lat_recv.at[d],
            device_id={"ord": target}, device_id_type=MESH,
        )

    def lat_forward(d):
        source = lax.rem(me_ord + n_ord - 2 * d, n_ord)
        return pltpu.make_async_remote_copy(
            src_ref=lat_rows(source), dst_ref=lat_rows(source),
            send_sem=lat_pass.at[d], recv_sem=lat_recv.at[half + d],
            device_id={"ord": mate}, device_id_type=MESH,
        )

    lat_own = pltpu.make_async_copy(lat, lat_rows(me_ord), in_sem.at[2, 2])

    def leaf_step(i):
        for copy in order_in(i):
            copy.wait()
        own[0, i] = lax.dot_general(
            coef[i], leaf[i], NT, preferred_element_type=jnp.float32
        ).astype(jnp.bfloat16)

    for i in range(WINDOW):
        leaf_step(i)
        level_copy(0, i).start()
    lat_in.wait()
    for d in range(half):
        lat_copy(d).start()
    lat_own.start()

    @pl.loop(WINDOW, orders)
    def _(i):
        leaf_step(i)

    interp_in.wait()

    def level_step(k, i):
        level_copy(k, i).wait_recv()
        mixed = lax.dot_general(
            own[k, i], interp[k, 0, i], NT, preferred_element_type=jnp.float32
        ) + lax.dot_general(
            came[k, i], interp[k, 1, i], NT, preferred_element_type=jnp.float32
        )
        own[k + 1, i] = mixed.astype(jnp.bfloat16)
        if k + 1 < levels:
            level_copy(k + 1, i).start()
        else:
            for d in range(1, n_ord):
                group_copy(i, d).start()
            own_copy(i).start()

    steps = orders + LEVEL_LAG * (levels - 1)

    @pl.loop(0, steps)
    def _(s):
        for k in range(levels):
            i = s - k * LEVEL_LAG

            @pl.when((i >= 0) & (i < orders))
            def _():
                level_step(k, i)
                if k == 0:
                    @pl.when(i + WINDOW < orders)
                    def _():
                        level_copy(0, i + WINDOW).start()

        @pl.when(s == orders - 1)
        def _():
            for d in range(1, half):
                lat_copy(d).wait_recv()
                lat_forward(d).start()

    lat_copy(0).wait_recv()
    for d in range(1, half):
        lat_forward(d).wait_recv()
    for d in range(half):
        lat_copy(d).wait_send()
    for d in range(1, half):
        lat_forward(d).wait_send()
    lat_own.wait()

    @pl.loop(0, orders)
    def _(i):
        for k in range(levels):
            level_copy(k, i).wait_send()
        for d in range(1, n_ord):
            group_copy(i, d).wait_recv()
            group_copy(i, d).wait_send()
        own_copy(i).wait()


def butterfly(flat, leaf_factors, interpolants, latitude_factors, parts, n_ord, n_blk):
    orders, columns, _ = flat.shape
    rank = leaf_factors.shape[1]
    levels = interpolants.shape[0]
    lats = latitude_factors.shape[1]
    group = columns // parts // n_ord
    any_spec = pl.BlockSpec(memory_space=pl.ANY)
    dma = pltpu.SemaphoreType.DMA
    return pl.pallas_call(
        functools.partial(butterfly_kernel, n_ord, n_blk),
        out_shape=(
            jax.ShapeDtypeStruct((n_ord * orders, parts, group, rank), jnp.bfloat16),
            jax.ShapeDtypeStruct((n_ord * orders, lats, rank), jnp.bfloat16),
        ),
        in_specs=[any_spec] * 4,
        out_specs=(any_spec, any_spec),
        scratch_shapes=[
            pltpu.VMEM(flat.shape, jnp.bfloat16),
            pltpu.VMEM(leaf_factors.shape, jnp.bfloat16),
            pltpu.VMEM(interpolants.shape, jnp.bfloat16),
            pltpu.VMEM(latitude_factors.shape, jnp.bfloat16),
            pltpu.VMEM((levels + 1, orders, columns, rank), jnp.bfloat16),
            pltpu.VMEM((levels, orders, columns, rank), jnp.bfloat16),
            dma((3, max(orders, 3))),
            dma((levels, orders)),
            dma((levels, orders)),
            dma((orders, n_ord)),
            dma((orders, n_ord)),
            dma((orders,)),
            dma((n_ord,)),
            dma((n_ord,)),
            dma((n_ord,)),
        ],
        compiler_params=pltpu.CompilerParams(collective_id=0, has_side_effects=True),
        name="butterfly",
    )(flat, leaf_factors, interpolants, latitude_factors)


def products_kernel(table_ref, rows_ref, lat_ref, out_ref, values, mixed):
    total, parts, group, rank = rows_ref.shape
    nlon, pairs, lanes = out_ref.shape
    depth = total * parts

    @pl.loop(0, total, unroll=4)
    def _(m):
        at = pl.multiple_of(m * parts * group, parts * group)
        values[pl.ds(at, parts * group), :] = lax.dot_general(
            rows_ref[m].reshape(parts * group, rank), lat_ref[m], NT,
            preferred_element_type=jnp.float32,
        )

    @pl.loop(0, pairs, unroll=2)
    def _(p):
        both = jnp.concatenate(
            [values[pl.ds(2 * p + h, depth, stride=group), :].astype(jnp.bfloat16) for h in range(2)],
            axis=1,
        )
        grid = jnp.dot(table_ref[...], both, preferred_element_type=jnp.float32)
        mixed[pl.ds(p, nlon, stride=pairs), :] = grid[:, :lanes] * grid[:, lanes:]

    @pl.loop(0, nlon // 16, unroll=2)
    def _(b):
        at = pl.multiple_of(b * 16 * pairs, 16 * pairs)
        out_ref[pl.ds(b * 16, 16)] = (
            mixed[pl.ds(at, 16 * pairs), :].astype(jnp.bfloat16).reshape(16, pairs, lanes)
        )


def products_of(table, rows, lat):
    total, parts, group, rank = rows.shape
    lats = lat.shape[1]
    pairs = group // 2
    nlon = table.shape[0]
    return pl.pallas_call(
        products_kernel,
        out_shape=jax.ShapeDtypeStruct((nlon, pairs, lats), jnp.bfloat16),
        grid=(lats // LANES,),
        in_specs=[
            pl.BlockSpec(table.shape, lambda t: (0, 0)),
            pl.BlockSpec(rows.shape, lambda t: (0, 0, 0, 0)),
            pl.BlockSpec((total, LANES, rank), lambda t: (0, t, 0)),
        ],
        out_specs=pl.BlockSpec((nlon, pairs, LANES), lambda t: (0, 0, t)),
        scratch_shapes=[
            pltpu.VMEM((total * parts * group, LANES), jnp.float32),
            pltpu.VMEM((nlon * pairs, LANES), jnp.float32),
        ],
        name="products",
    )(table, rows, lat)


def per_device(coefficients, leaf_factors, level_interpolants, latitude_factors, order_ids):
    orders_here, parts, fields, leaf = coefficients.shape
    flat = coefficients.reshape(orders_here, parts * fields, leaf)
    rows, lat = butterfly(
        flat, leaf_factors, level_interpolants, latitude_factors, parts,
        lax.axis_size("ord"), lax.axis_size("blk"),
    )
    return products_of(synthesis_table(order_ids, NLON, PERIOD), rows, lat)


def solution(mesh):
    in_specs = (
        P("ord", None, None, "blk"),
        P("ord", None, "blk"),
        P(None, None, "ord", None, "blk"),
        P("ord", "blk", None),
        P(),
    )
    out_specs = P(None, "ord", "blk")
    return jax.shard_map(
        per_device, mesh=mesh, in_specs=in_specs, out_specs=out_specs, check_vma=False
    )
```

```python
import functools
import math

import jax
import jax.numpy as jnp
from jax import lax
from jax.experimental import pallas as pl
from jax.experimental.pallas import tpu as pltpu
from jax.sharding import PartitionSpec as P

PERIOD = 16384
NLON = 256
LANES = 128
WINDOW = 2
LEVEL_LAG = 1
MESH = pl.DeviceIdType.MESH
NT = (((1,), (1,)), ((), ()))


def synthesis_table(order_ids, count, period):
    steps = jnp.arange(count, dtype=jnp.int32)
    phase = (steps[:, None] * order_ids[None, :] % period).astype(jnp.float32) * (
        2.0 * math.pi / period
    )
    weight = jnp.where(order_ids == 0, 1.0, 2.0).astype(jnp.float32)[None, :]
    table = jnp.stack([weight * jnp.cos(phase), -weight * jnp.sin(phase)], axis=2)
    return table.astype(jnp.bfloat16).reshape(count, -1)


def butterfly_kernel(
    n_ord, n_blk, coef_hbm, leaf_hbm, interp_hbm, lat_hbm,
    rows_out, lat_out,
    coef, leaf, interp, lat, own, came,
    in_sem, level_send, level_recv, group_send, group_recv, own_sem,
    lat_send, lat_recv, lat_pass,
):
    me_ord, me_blk = lax.axis_index("ord"), lax.axis_index("blk")
    orders, columns, _ = coef.shape
    levels = interp.shape[0]
    parts, _, group, rank = rows_out.shape[1], None, rows_out.shape[2], rows_out.shape[3]

    lat_in = pltpu.make_async_copy(lat_hbm, lat, in_sem.at[2, 0])
    interp_in = pltpu.make_async_copy(interp_hbm, interp, in_sem.at[2, 1])

    def order_in(i):
        return (
            pltpu.make_async_copy(coef_hbm.at[i], coef.at[i], in_sem.at[0, i]),
            pltpu.make_async_copy(leaf_hbm.at[i], leaf.at[i], in_sem.at[1, i]),
        )

    for i in range(orders):
        for copy in order_in(i):
            copy.start()
        if i == 1:
            lat_in.start()
            interp_in.start()

    barrier = pltpu.get_barrier_semaphore()
    partners = [me_blk ^ (n_blk >> (k + 1)) for k in range(levels)]
    for k in range(levels):
        pl.semaphore_signal(barrier, inc=1, device_id={"blk": partners[k]}, device_id_type=MESH)
    peers = [lax.rem(me_ord + d, n_ord) for d in range(1, n_ord)]
    for peer in peers:
        pl.semaphore_signal(barrier, inc=1, device_id={"ord": peer}, device_id_type=MESH)
    pl.semaphore_wait(barrier, levels + n_ord - 1)

    def level_copy(k, i):
        return pltpu.make_async_remote_copy(
            src_ref=own.at[k, i], dst_ref=came.at[k, i],
            send_sem=level_send.at[k, i], recv_sem=level_recv.at[k, i],
            device_id={"blk": partners[k]}, device_id_type=MESH,
        )

    def group_copy(i, d):
        peer = lax.rem(me_ord + d, n_ord)
        return pltpu.make_async_remote_copy(
            src_ref=own_groups(i, peer), dst_ref=rows_out.at[me_ord * orders + i],
            send_sem=group_send.at[i, d], recv_sem=group_recv.at[i, d],
            device_id={"ord": peer}, device_id_type=MESH,
        )

    def own_groups(i, g):
        return own.at[levels, i].reshape(parts, n_ord, group, rank).at[:, g]

    def own_copy(i):
        return pltpu.make_async_copy(
            own_groups(i, me_ord), rows_out.at[me_ord * orders + i], own_sem.at[i]
        )

    def lat_rows(o):
        return lat_out.at[pl.ds(o * orders, orders)]

    half = n_ord // 2
    mate = me_ord ^ 1

    def lat_copy(d):
        target = mate if d == 0 else lax.rem(me_ord + 2 * d, n_ord)
        return pltpu.make_async_remote_copy(
            src_ref=lat, dst_ref=lat_rows(me_ord),
            send_sem=lat_send.at[d], recv_sem=lat_recv.at[d],
            device_id={"ord": target}, device_id_type=MESH,
        )

    def lat_forward(d):
        source = lax.rem(me_ord + n_ord - 2 * d, n_ord)
        return pltpu.make_async_remote_copy(
            src_ref=lat_rows(source), dst_ref=lat_rows(source),
            send_sem=lat_pass.at[d], recv_sem=lat_recv.at[half + d],
            device_id={"ord": mate}, device_id_type=MESH,
        )

    lat_own = pltpu.make_async_copy(lat, lat_rows(me_ord), in_sem.at[2, 2])

    def leaf_step(i):
        for copy in order_in(i):
            copy.wait()
        own[0, i] = lax.dot_general(
            coef[i], leaf[i], NT, preferred_element_type=jnp.float32
        ).astype(jnp.bfloat16)

    for i in range(WINDOW):
        leaf_step(i)
        level_copy(0, i).start()
    lat_in.wait()
    for d in range(half):
        lat_copy(d).start()
    lat_own.start()

    @pl.loop(WINDOW, orders)
    def _(i):
        leaf_step(i)

    interp_in.wait()

    def level_step(k, i):
        level_copy(k, i).wait_recv()
        mixed = lax.dot_general(
            own[k, i], interp[k, 0, i], NT, preferred_element_type=jnp.float32
        ) + lax.dot_general(
            came[k, i], interp[k, 1, i], NT, preferred_element_type=jnp.float32
        )
        own[k + 1, i] = mixed.astype(jnp.bfloat16)
        if k + 1 < levels:
            level_copy(k + 1, i).start()
        else:
            for d in range(1, n_ord):
                group_copy(i, d).start()
            own_copy(i).start()

    steps = orders + LEVEL_LAG * (levels - 1)

    @pl.loop(0, steps)
    def _(s):
        for k in range(levels):
            i = s - k * LEVEL_LAG

            @pl.when((i >= 0) & (i < orders))
            def _():
                level_step(k, i)
                if k == 0:
                    @pl.when(i + WINDOW < orders)
                    def _():
                        level_copy(0, i + WINDOW).start()

        @pl.when(s == orders - 1)
        def _():
            for d in range(1, half):
                lat_copy(d).wait_recv()
                lat_forward(d).start()

    lat_copy(0).wait_recv()
    for d in range(1, half):
        lat_forward(d).wait_recv()
    for d in range(half):
        lat_copy(d).wait_send()
    for d in range(1, half):
        lat_forward(d).wait_send()
    lat_own.wait()

    @pl.loop(0, orders)
    def _(i):
        for k in range(levels):
            level_copy(k, i).wait_send()
        for d in range(1, n_ord):
            group_copy(i, d).wait_recv()
            group_copy(i, d).wait_send()
        own_copy(i).wait()


def butterfly(flat, leaf_factors, interpolants, latitude_factors, parts, n_ord, n_blk):
    orders, columns, _ = flat.shape
    rank = leaf_factors.shape[1]
    levels = interpolants.shape[0]
    lats = latitude_factors.shape[1]
    group = columns // parts // n_ord
    any_spec = pl.BlockSpec(memory_space=pl.ANY)
    dma = pltpu.SemaphoreType.DMA
    return pl.pallas_call(
        functools.partial(butterfly_kernel, n_ord, n_blk),
        out_shape=(
            jax.ShapeDtypeStruct((n_ord * orders, parts, group, rank), jnp.bfloat16),
            jax.ShapeDtypeStruct((n_ord * orders, lats, rank), jnp.bfloat16),
        ),
        in_specs=[any_spec] * 4,
        out_specs=(any_spec, any_spec),
        scratch_shapes=[
            pltpu.VMEM(flat.shape, jnp.bfloat16),
            pltpu.VMEM(leaf_factors.shape, jnp.bfloat16),
            pltpu.VMEM(interpolants.shape, jnp.bfloat16),
            pltpu.VMEM(latitude_factors.shape, jnp.bfloat16),
            pltpu.VMEM((levels + 1, orders, columns, rank), jnp.bfloat16),
            pltpu.VMEM((levels, orders, columns, rank), jnp.bfloat16),
            dma((3, max(orders, 3))),
            dma((levels, orders)),
            dma((levels, orders)),
            dma((orders, n_ord)),
            dma((orders, n_ord)),
            dma((orders,)),
            dma((n_ord,)),
            dma((n_ord,)),
            dma((n_ord,)),
        ],
        compiler_params=pltpu.CompilerParams(collective_id=0, has_side_effects=True),
        name="butterfly",
    )(flat, leaf_factors, interpolants, latitude_factors)


def products_kernel(table_ref, rows_ref, lat_ref, out_ref, values, mixed):
    total, parts, group, rank = rows_ref.shape
    nlon, pairs, lanes = out_ref.shape
    depth = total * parts

    @pl.loop(0, total, unroll=4)
    def _(m):
        values[pl.ds(m * parts, parts)] = lax.dot_general(
            rows_ref[m].reshape(parts * group, rank), lat_ref[m], NT,
            preferred_element_type=jnp.float32,
        ).reshape(parts, group, lanes).astype(jnp.bfloat16)

    @pl.loop(0, group // 16)
    def _(q):
        fields = jnp.transpose(values[:, pl.ds(pl.multiple_of(q * 16, 16), 16), :], (1, 0, 2))
        for h in range(8):
            both = jnp.concatenate([fields[2 * h], fields[2 * h + 1]], axis=1)
            grid = jnp.dot(table_ref[...], both, preferred_element_type=jnp.float32)
            mixed[q * 8 + h] = (grid[:, :lanes] * grid[:, lanes:]).astype(jnp.bfloat16)

    @pl.loop(0, nlon // 16)
    def _(b):
        at = pl.ds(pl.multiple_of(b * 16, 16), 16)
        out_ref[at] = jnp.transpose(mixed[:, at, :], (1, 0, 2))


def products_of(table, rows, lat):
    total, parts, group, rank = rows.shape
    lats = lat.shape[1]
    pairs = group // 2
    nlon = table.shape[0]
    return pl.pallas_call(
        products_kernel,
        out_shape=jax.ShapeDtypeStruct((nlon, pairs, lats), jnp.bfloat16),
        grid=(lats // LANES,),
        in_specs=[
            pl.BlockSpec(table.shape, lambda t: (0, 0)),
            pl.BlockSpec(rows.shape, lambda t: (0, 0, 0, 0)),
            pl.BlockSpec((total, LANES, rank), lambda t: (0, t, 0)),
        ],
        out_specs=pl.BlockSpec((nlon, pairs, LANES), lambda t: (0, 0, t)),
        scratch_shapes=[
            pltpu.VMEM((total * parts, group, LANES), jnp.bfloat16),
            pltpu.VMEM((pairs, nlon, LANES), jnp.bfloat16),
        ],
        name="products",
    )(table, rows, lat)


def per_device(coefficients, leaf_factors, level_interpolants, latitude_factors, order_ids):
    orders_here, parts, fields, leaf = coefficients.shape
    flat = coefficients.reshape(orders_here, parts * fields, leaf)
    rows, lat = butterfly(
        flat, leaf_factors, level_interpolants, latitude_factors, parts,
        lax.axis_size("ord"), lax.axis_size("blk"),
    )
    return products_of(synthesis_table(order_ids, NLON, PERIOD), rows, lat)


def solution(mesh):
    in_specs = (
        P("ord", None, None, "blk"),
        P("ord", None, "blk"),
        P(None, None, "ord", None, "blk"),
        P("ord", "blk", None),
        P(),
    )
    out_specs = P(None, "ord", "blk")
    return jax.shard_map(
        per_device, mesh=mesh, in_specs=in_specs, out_specs=out_specs, check_vma=False
    )
```

```python
import functools
import math

import jax
import jax.numpy as jnp
from jax import lax
from jax.experimental import pallas as pl
from jax.experimental.pallas import tpu as pltpu
from jax.sharding import PartitionSpec as P

PERIOD = 16384
NLON = 256
LANES = 128
WINDOW = 4
LEVEL_LAG = 3
MESH = pl.DeviceIdType.MESH
NT = (((1,), (1,)), ((), ()))


def synthesis_table(order_ids, count, period):
    steps = lax.broadcasted_iota(jnp.int32, (count, order_ids.shape[1]), 0)
    phase = lax.rem(steps * order_ids, period).astype(jnp.float32) * (2.0 * math.pi / period)
    weight = jnp.where(order_ids == 0, 1.0, 2.0).astype(jnp.float32)
    table = jnp.concatenate([weight * jnp.cos(phase), -weight * jnp.sin(phase)], axis=1)
    return table.astype(jnp.bfloat16)


def butterfly_kernel(
    n_ord, n_blk, coef_hbm, leaf_hbm, interp_hbm, lat_hbm, ids_ref,
    rows_out, lat_out, table_ref,
    coef, leaf, interp, lat, own, came,
    in_sem, level_send, level_recv, group_send, group_recv, own_sem,
    lat_send, lat_recv, lat_pass,
):
    me_ord, me_blk = lax.axis_index("ord"), lax.axis_index("blk")
    orders, parts, _, _ = coef.shape
    levels = interp.shape[0]
    chunks = orders * parts
    group = rows_out.shape[2]

    lat_in = pltpu.make_async_copy(lat_hbm, lat, in_sem.at[2, 0])
    interp_in = pltpu.make_async_copy(interp_hbm, interp, in_sem.at[2, 1])

    def order_in(i):
        return (
            pltpu.make_async_copy(coef_hbm.at[i], coef.at[i], in_sem.at[0, i]),
            pltpu.make_async_copy(leaf_hbm.at[i], leaf.at[i], in_sem.at[1, i]),
        )

    for i in range(orders):
        for copy in order_in(i):
            copy.start()
        if i == 1:
            interp_in.start()
            lat_in.start()

    barrier = pltpu.get_barrier_semaphore()
    partners = [me_blk ^ (n_blk >> (k + 1)) for k in range(levels)]
    for k in range(levels):
        pl.semaphore_signal(barrier, inc=1, device_id={"blk": partners[k]}, device_id_type=MESH)
    for d in range(1, n_ord):
        pl.semaphore_signal(
            barrier, inc=1, device_id={"ord": lax.rem(me_ord + d, n_ord)}, device_id_type=MESH
        )

    def leaf_step(c):
        i, part = c // parts, lax.rem(c, parts)

        @pl.when(part == 0)
        def _():
            for copy in order_in(i):
                copy.wait()

        own[0, c] = lax.dot_general(
            coef[i, part], leaf[i], NT, preferred_element_type=jnp.float32
        ).astype(jnp.bfloat16)

    leaf_step(0)
    pl.semaphore_wait(barrier, levels + n_ord - 1)

    def level_copy(k, c):
        return pltpu.make_async_remote_copy(
            src_ref=own.at[k, c], dst_ref=came.at[k, c],
            send_sem=level_send.at[k, c], recv_sem=level_recv.at[k, c],
            device_id={"blk": partners[k]}, device_id_type=MESH,
        )

    def group_rows(c, g):
        return own.at[levels, c, pl.ds(pl.multiple_of(g * group, group), group)]

    def landing(c):
        return rows_out.at[me_ord * orders + c // parts, lax.rem(c, parts)]

    def group_copy(c, d):
        peer = lax.rem(me_ord + d, n_ord)
        return pltpu.make_async_remote_copy(
            src_ref=group_rows(c, peer), dst_ref=landing(c),
            send_sem=group_send.at[c, d], recv_sem=group_recv.at[c, d],
            device_id={"ord": peer}, device_id_type=MESH,
        )

    def own_copy(c):
        return pltpu.make_async_copy(group_rows(c, me_ord), landing(c), own_sem.at[c])

    def lat_rows(o):
        return lat_out.at[pl.ds(o * orders, orders)]

    half = n_ord // 2
    mate = me_ord ^ 1

    def lat_copy(d):
        target = mate if d == 0 else lax.rem(me_ord + 2 * d, n_ord)
        return pltpu.make_async_remote_copy(
            src_ref=lat, dst_ref=lat_rows(me_ord),
            send_sem=lat_send.at[d], recv_sem=lat_recv.at[d],
            device_id={"ord": target}, device_id_type=MESH,
        )

    def lat_forward(d):
        source = lax.rem(me_ord + n_ord - 2 * d, n_ord)
        return pltpu.make_async_remote_copy(
            src_ref=lat_rows(source), dst_ref=lat_rows(source),
            send_sem=lat_pass.at[d], recv_sem=lat_recv.at[half + d],
            device_id={"ord": mate}, device_id_type=MESH,
        )

    lat_own = pltpu.make_async_copy(lat, lat_rows(me_ord), in_sem.at[2, 2])

    level_copy(0, 0).start()

    @pl.loop(1, WINDOW)
    def _(c):
        leaf_step(c)
        level_copy(0, c).start()

    lat_in.wait()
    for d in range(half):
        lat_copy(d).start()
    lat_own.start()
    interp_in.wait()
    table_ref[...] = synthesis_table(ids_ref[...], table_ref.shape[0], PERIOD)

    def level_step(k, c):
        i = c // parts
        level_copy(k, c).wait_recv()
        mixed = lax.dot_general(
            own[k, c], interp[k, 0, i], NT, preferred_element_type=jnp.float32
        ) + lax.dot_general(
            came[k, c], interp[k, 1, i], NT, preferred_element_type=jnp.float32
        )
        own[k + 1, c] = mixed.astype(jnp.bfloat16)
        if k + 1 < levels:
            level_copy(k + 1, c).start()
        else:
            for d in range(1, n_ord):
                group_copy(c, d).start()
            own_copy(c).start()

    @pl.loop(0, chunks + LEVEL_LAG * (levels - 1))
    def _(s):
        @pl.when(s + WINDOW < chunks)
        def _():
            leaf_step(s + WINDOW)

        for k in range(levels):
            c = s - k * LEVEL_LAG

            @pl.when((c >= 0) & (c < chunks))
            def _():
                level_step(k, c)

            if k == 0:
                @pl.when(s + WINDOW < chunks)
                def _():
                    level_copy(0, s + WINDOW).start()

        @pl.when(s == chunks - 3)
        def _():
            for d in range(1, half):
                lat_copy(d).wait_recv()
                lat_forward(d).start()

    lat_copy(0).wait_recv()
    for d in range(1, half):
        lat_forward(d).wait_recv()
    for d in range(half):
        lat_copy(d).wait_send()
    for d in range(1, half):
        lat_forward(d).wait_send()
    lat_own.wait()

    @pl.loop(0, chunks)
    def _(c):
        for k in range(levels):
            level_copy(k, c).wait_send()
        for d in range(1, n_ord):
            group_copy(c, d).wait_recv()
            group_copy(c, d).wait_send()
        own_copy(c).wait()


def butterfly(coefficients, leaf_factors, interpolants, latitude_factors, order_ids, n_ord, n_blk):
    orders, parts, fields, _ = coefficients.shape
    rank = leaf_factors.shape[1]
    levels = interpolants.shape[0]
    lats = latitude_factors.shape[1]
    chunks = orders * parts
    total = n_ord * orders
    any_spec = pl.BlockSpec(memory_space=pl.ANY)
    vmem_spec = pl.BlockSpec(memory_space=pltpu.VMEM)
    dma = pltpu.SemaphoreType.DMA
    return pl.pallas_call(
        functools.partial(butterfly_kernel, n_ord, n_blk),
        out_shape=(
            jax.ShapeDtypeStruct((total, parts, fields // n_ord, rank), jnp.bfloat16),
            jax.ShapeDtypeStruct((total, lats, rank), jnp.bfloat16),
            jax.ShapeDtypeStruct((NLON, parts * total), jnp.bfloat16),
        ),
        in_specs=[any_spec] * 4 + [vmem_spec],
        out_specs=(any_spec, any_spec, vmem_spec),
        scratch_shapes=[
            pltpu.VMEM(coefficients.shape, jnp.bfloat16),
            pltpu.VMEM(leaf_factors.shape, jnp.bfloat16),
            pltpu.VMEM(interpolants.shape, jnp.bfloat16),
            pltpu.VMEM(latitude_factors.shape, jnp.bfloat16),
            pltpu.VMEM((levels + 1, chunks, fields, rank), jnp.bfloat16),
            pltpu.VMEM((levels, chunks, fields, rank), jnp.bfloat16),
            dma((3, max(orders, 3))),
            dma((levels, chunks)),
            dma((levels, chunks)),
            dma((chunks, n_ord)),
            dma((chunks, n_ord)),
            dma((chunks,)),
            dma((n_ord,)),
            dma((n_ord,)),
            dma((n_ord,)),
        ],
        compiler_params=pltpu.CompilerParams(collective_id=0, has_side_effects=True),
        name="butterfly",
    )(coefficients, leaf_factors, interpolants, latitude_factors, order_ids[None, :])


def products_kernel(table_ref, rows_ref, lat_ref, out_ref, values, mixed):
    total, parts, group, rank = rows_ref.shape
    nlon, pairs, lanes = out_ref.shape
    depth = total * parts

    @pl.loop(0, total, unroll=8)
    def _(m):
        mapped = lax.dot_general(
            rows_ref[m].reshape(parts * group, rank), lat_ref[m], NT,
            preferred_element_type=jnp.float32,
        ).reshape(parts, group, lanes).astype(jnp.bfloat16)
        for part in range(parts):
            values[part * total + m] = mapped[part]

    @pl.loop(0, group // 16, unroll=True)
    def _(q):
        fields = jnp.transpose(values[:, pl.ds(pl.multiple_of(q * 16, 16), 16), :], (1, 0, 2))
        for h in range(8):
            both = jnp.concatenate([fields[2 * h], fields[2 * h + 1]], axis=1)
            grid = jnp.dot(table_ref[...], both, preferred_element_type=jnp.float32)
            mixed[q * 8 + h] = (grid[:, :lanes] * grid[:, lanes:]).astype(jnp.bfloat16)

    @pl.loop(0, nlon // 16, unroll=4)
    def _(b):
        at = pl.ds(pl.multiple_of(b * 16, 16), 16)
        out_ref[at] = jnp.transpose(mixed[:, at, :], (1, 0, 2))


def products_of(table, rows, lat):
    total, parts, group, rank = rows.shape
    lats = lat.shape[1]
    pairs = group // 2
    nlon = table.shape[0]
    return pl.pallas_call(
        products_kernel,
        out_shape=jax.ShapeDtypeStruct((nlon, pairs, lats), jnp.bfloat16),
        grid=(lats // LANES,),
        in_specs=[
            pl.BlockSpec(table.shape, lambda t: (0, 0)),
            pl.BlockSpec(rows.shape, lambda t: (0, 0, 0, 0)),
            pl.BlockSpec((total, LANES, rank), lambda t: (0, t, 0)),
        ],
        out_specs=pl.BlockSpec((nlon, pairs, LANES), lambda t: (0, 0, t)),
        scratch_shapes=[
            pltpu.VMEM((total * parts, group, LANES), jnp.bfloat16),
            pltpu.VMEM((pairs, nlon, LANES), jnp.bfloat16),
        ],
        name="products",
    )(table, rows, lat)


def per_device(coefficients, leaf_factors, level_interpolants, latitude_factors, order_ids):
    rows, lat, table = butterfly(
        coefficients, leaf_factors, level_interpolants, latitude_factors, order_ids,
        lax.axis_size("ord"), lax.axis_size("blk"),
    )
    return products_of(table, rows, lat)


def solution(mesh):
    in_specs = (
        P("ord", None, None, "blk"),
        P("ord", None, "blk"),
        P(None, None, "ord", None, "blk"),
        P("ord", "blk", None),
        P(),
    )
    out_specs = P(None, "ord", "blk")
    return jax.shard_map(
        per_device, mesh=mesh, in_specs=in_specs, out_specs=out_specs, check_vma=False
    )
```

```python
import functools
import math

import jax
import jax.numpy as jnp
from jax import lax
from jax.experimental import pallas as pl
from jax.experimental.pallas import tpu as pltpu
from jax.sharding import PartitionSpec as P

PERIOD = 16384
NLON = 256
LANES = 128
WINDOW = 4
LEVEL_LAG = 3
MESH = pl.DeviceIdType.MESH
NT = (((1,), (1,)), ((), ()))


def synthesis_table(order_ids, count, period):
    steps = lax.broadcasted_iota(jnp.int32, (count, order_ids.shape[1]), 0)
    phase = lax.rem(steps * order_ids, period).astype(jnp.float32) * (2.0 * math.pi / period)
    weight = jnp.where(order_ids == 0, 1.0, 2.0).astype(jnp.float32)
    table = jnp.concatenate([weight * jnp.cos(phase), -weight * jnp.sin(phase)], axis=1)
    return table.astype(jnp.bfloat16)


def butterfly_kernel(
    n_ord, n_blk, coef_hbm, leaf_hbm, interp_hbm, lat_hbm, ids_ref,
    rows_out, lat_out, table_ref,
    coef, leaf, interp, lat, own, came,
    in_sem, level_send, level_recv, group_send, group_recv, own_sem,
    lat_send, lat_recv, lat_pass,
):
    me_ord, me_blk = lax.axis_index("ord"), lax.axis_index("blk")
    orders, parts, _, _ = coef.shape
    levels = interp.shape[0]
    chunks = orders * parts
    group = rows_out.shape[2]

    lat_in = pltpu.make_async_copy(lat_hbm, lat, in_sem.at[2, 0])
    interp_in = pltpu.make_async_copy(interp_hbm, interp, in_sem.at[2, 1])

    def order_in(i):
        return (
            pltpu.make_async_copy(coef_hbm.at[i], coef.at[i], in_sem.at[0, i]),
            pltpu.make_async_copy(leaf_hbm.at[i], leaf.at[i], in_sem.at[1, i]),
        )

    for i in range(orders):
        for copy in order_in(i):
            copy.start()
        if i == 1:
            interp_in.start()
            lat_in.start()

    barrier = pltpu.get_barrier_semaphore()
    partners = [me_blk ^ (n_blk >> (k + 1)) for k in range(levels)]
    for k in range(levels):
        pl.semaphore_signal(barrier, inc=1, device_id={"blk": partners[k]}, device_id_type=MESH)
    for d in range(1, n_ord):
        pl.semaphore_signal(
            barrier, inc=1, device_id={"ord": lax.rem(me_ord + d, n_ord)}, device_id_type=MESH
        )

    def leaf_step(c):
        i, part = c // parts, lax.rem(c, parts)

        @pl.when(part == 0)
        def _():
            for copy in order_in(i):
                copy.wait()

        own[0, c] = lax.dot_general(
            coef[i, part], leaf[i], NT, preferred_element_type=jnp.float32
        ).astype(jnp.bfloat16)

    leaf_step(0)
    pl.semaphore_wait(barrier, levels + n_ord - 1)

    def level_copy(k, c):
        return pltpu.make_async_remote_copy(
            src_ref=own.at[k, c], dst_ref=came.at[k, c],
            send_sem=level_send.at[k, c], recv_sem=level_recv.at[k, c],
            device_id={"blk": partners[k]}, device_id_type=MESH,
        )

    def group_rows(c, g):
        return own.at[levels, c, pl.ds(pl.multiple_of(g * group, group), group)]

    def landing(c):
        return rows_out.at[me_ord * orders + c // parts, lax.rem(c, parts)]

    def group_copy(c, d):
        peer = lax.rem(me_ord + d, n_ord)
        return pltpu.make_async_remote_copy(
            src_ref=group_rows(c, peer), dst_ref=landing(c),
            send_sem=group_send.at[c, d], recv_sem=group_recv.at[c, d],
            device_id={"ord": peer}, device_id_type=MESH,
        )

    def own_copy(c):
        return pltpu.make_async_copy(group_rows(c, me_ord), landing(c), own_sem.at[c])

    def lat_rows(o):
        return lat_out.at[pl.ds(o * orders, orders)]

    half = n_ord // 2
    mate = me_ord ^ 1

    def lat_copy(d):
        target = mate if d == 0 else lax.rem(me_ord + 2 * d, n_ord)
        return pltpu.make_async_remote_copy(
            src_ref=lat, dst_ref=lat_rows(me_ord),
            send_sem=lat_send.at[d], recv_sem=lat_recv.at[d],
            device_id={"ord": target}, device_id_type=MESH,
        )

    def lat_forward(d):
        source = lax.rem(me_ord + n_ord - 2 * d, n_ord)
        return pltpu.make_async_remote_copy(
            src_ref=lat_rows(source), dst_ref=lat_rows(source),
            send_sem=lat_pass.at[d], recv_sem=lat_recv.at[half + d],
            device_id={"ord": mate}, device_id_type=MESH,
        )

    lat_own = pltpu.make_async_copy(lat, lat_rows(me_ord), in_sem.at[2, 2])

    level_copy(0, 0).start()

    @pl.loop(1, WINDOW)
    def _(c):
        leaf_step(c)
        level_copy(0, c).start()

    lat_in.wait()
    for d in range(half):
        lat_copy(d).start()
    lat_own.start()
    interp_in.wait()
    table_ref[...] = synthesis_table(ids_ref[...], table_ref.shape[0], PERIOD)

    def level_step(k, c):
        i = c // parts
        level_copy(k, c).wait_recv()
        mixed = lax.dot_general(
            own[k, c], interp[k, 0, i], NT, preferred_element_type=jnp.float32
        ) + lax.dot_general(
            came[k, c], interp[k, 1, i], NT, preferred_element_type=jnp.float32
        )
        own[k + 1, c] = mixed.astype(jnp.bfloat16)
        if k + 1 < levels:
            level_copy(k + 1, c).start()
        else:
            for d in range(1, n_ord):
                group_copy(c, d).start()
            own_copy(c).start()

    @pl.loop(0, chunks + LEVEL_LAG * (levels - 1))
    def _(s):
        @pl.when(s + WINDOW < chunks)
        def _():
            leaf_step(s + WINDOW)

        for k in range(levels):
            c = s - k * LEVEL_LAG

            @pl.when((c >= 0) & (c < chunks))
            def _():
                level_step(k, c)

            if k == 0:
                @pl.when(s + WINDOW < chunks)
                def _():
                    level_copy(0, s + WINDOW).start()

        @pl.when(s == chunks - 3)
        def _():
            for d in range(1, half):
                lat_copy(d).wait_recv()
                lat_forward(d).start()

    lat_copy(0).wait_recv()
    for d in range(1, half):
        lat_forward(d).wait_recv()
    for d in range(half):
        lat_copy(d).wait_send()
    for d in range(1, half):
        lat_forward(d).wait_send()
    lat_own.wait()

    @pl.loop(0, chunks)
    def _(c):
        for k in range(levels):
            level_copy(k, c).wait_send()
        for d in range(1, n_ord):
            group_copy(c, d).wait_recv()
            group_copy(c, d).wait_send()
        own_copy(c).wait()


def butterfly(coefficients, leaf_factors, interpolants, latitude_factors, order_ids, n_ord, n_blk):
    orders, parts, fields, _ = coefficients.shape
    rank = leaf_factors.shape[1]
    levels = interpolants.shape[0]
    lats = latitude_factors.shape[1]
    chunks = orders * parts
    total = n_ord * orders
    any_spec = pl.BlockSpec(memory_space=pl.ANY)
    vmem_spec = pl.BlockSpec(memory_space=pltpu.VMEM)
    dma = pltpu.SemaphoreType.DMA
    return pl.pallas_call(
        functools.partial(butterfly_kernel, n_ord, n_blk),
        out_shape=(
            jax.ShapeDtypeStruct((total, parts, fields // n_ord, rank), jnp.bfloat16),
            jax.ShapeDtypeStruct((total, lats, rank), jnp.bfloat16),
            jax.ShapeDtypeStruct((NLON, parts * total), jnp.bfloat16),
        ),
        in_specs=[any_spec] * 4 + [vmem_spec],
        out_specs=(any_spec, any_spec, vmem_spec),
        scratch_shapes=[
            pltpu.VMEM(coefficients.shape, jnp.bfloat16),
            pltpu.VMEM(leaf_factors.shape, jnp.bfloat16),
            pltpu.VMEM(interpolants.shape, jnp.bfloat16),
            pltpu.VMEM(latitude_factors.shape, jnp.bfloat16),
            pltpu.VMEM((levels + 1, chunks, fields, rank), jnp.bfloat16),
            pltpu.VMEM((levels, chunks, fields, rank), jnp.bfloat16),
            dma((3, max(orders, 3))),
            dma((levels, chunks)),
            dma((levels, chunks)),
            dma((chunks, n_ord)),
            dma((chunks, n_ord)),
            dma((chunks,)),
            dma((n_ord,)),
            dma((n_ord,)),
            dma((n_ord,)),
        ],
        compiler_params=pltpu.CompilerParams(collective_id=0, has_side_effects=True),
        name="butterfly",
    )(coefficients, leaf_factors, interpolants, latitude_factors, order_ids[None, :])


def products_kernel(table_ref, rows_ref, lat_ref, out_ref, values, mixed):
    total, parts, group, rank = rows_ref.shape
    nlon, pairs, lanes = out_ref.shape
    depth = total * parts

    @pl.loop(0, total, unroll=32)
    def _(m):
        mapped = lax.dot_general(
            rows_ref[m].reshape(parts * group, rank), lat_ref[m], NT,
            preferred_element_type=jnp.float32,
        ).reshape(parts, group, lanes).astype(jnp.bfloat16)
        for part in range(parts):
            values[part * total + m] = mapped[part]

    @pl.loop(0, group // 16, unroll=True)
    def _(q):
        fields = jnp.transpose(values[:, pl.ds(pl.multiple_of(q * 16, 16), 16), :], (1, 0, 2))
        for h in range(8):
            both = jnp.concatenate([fields[2 * h], fields[2 * h + 1]], axis=1)
            grid = jnp.dot(table_ref[...], both, preferred_element_type=jnp.float32)
            mixed[q * 8 + h] = (grid[:, :lanes] * grid[:, lanes:]).astype(jnp.bfloat16)

    @pl.loop(0, nlon // 16, unroll=4)
    def _(b):
        at = pl.ds(pl.multiple_of(b * 16, 16), 16)
        out_ref[at] = jnp.transpose(mixed[:, at, :], (1, 0, 2))


def products_of(table, rows, lat):
    total, parts, group, rank = rows.shape
    lats = lat.shape[1]
    pairs = group // 2
    nlon = table.shape[0]
    return pl.pallas_call(
        products_kernel,
        out_shape=jax.ShapeDtypeStruct((nlon, pairs, lats), jnp.bfloat16),
        grid=(lats // LANES,),
        in_specs=[
            pl.BlockSpec(table.shape, lambda t: (0, 0)),
            pl.BlockSpec(rows.shape, lambda t: (0, 0, 0, 0)),
            pl.BlockSpec((total, LANES, rank), lambda t: (0, t, 0)),
        ],
        out_specs=pl.BlockSpec((nlon, pairs, LANES), lambda t: (0, 0, t)),
        scratch_shapes=[
            pltpu.VMEM((total * parts, group, LANES), jnp.bfloat16),
            pltpu.VMEM((pairs, nlon, LANES), jnp.bfloat16),
        ],
        name="products",
    )(table, rows, lat)


def per_device(coefficients, leaf_factors, level_interpolants, latitude_factors, order_ids):
    rows, lat, table = butterfly(
        coefficients, leaf_factors, level_interpolants, latitude_factors, order_ids,
        lax.axis_size("ord"), lax.axis_size("blk"),
    )
    return products_of(table, rows, lat)


def solution(mesh):
    in_specs = (
        P("ord", None, None, "blk"),
        P("ord", None, "blk"),
        P(None, None, "ord", None, "blk"),
        P("ord", "blk", None),
        P(),
    )
    out_specs = P(None, "ord", "blk")
    return jax.shard_map(
        per_device, mesh=mesh, in_specs=in_specs, out_specs=out_specs, check_vma=False
    )
```
